32 devices in a mesh: expert: 16 (over z, y, x), dp: 2 (over core).
Axes of the slice: x: 2, y: 2, z: 4, core: 2. Of those that a mesh axis runs over, the one named last changes fastest.
Arguments:
- tokens: bfloat16 [2048, 2048], P(('expert', 'dp')), may hold values from -6 to 6
- expert_ids: int32 [2048, 8], P(('expert', 'dp')), may hold values from 0 to 15, all different within a row; in each aligned block of 64 rows (0 to 63, 64 to 127, ...) at most 48 rows name the same one
- gate_probs: float32 [2048, 8], P(('expert', 'dp')), may hold values from 0.05 to 1
- swap_flags: int32 [8], replicated, may hold values from 0 to 1, as said below
- w_gate: bfloat16 [16, 2048, 768], P('expert', 'dp'), may hold values from -0.125 to 0.125
- w_up: bfloat16 [16, 2048, 768], P('expert', 'dp'), may hold values from -0.125 to 0.125
- w_down: bfloat16 [16, 768, 2048], P('expert', None, 'dp'), may hold values from -0.21875 to 0.21875
Outputs:
- moe_out: bfloat16 [2048, 2048], P(('expert', 'dp'))
The draws below stay inside these ranges and needn't reach their ends.
Inputs may be any that keep to these rules, and one draw needn't show every extreme that they name: `expert_ids`: each row names 8 different experts. Within the 64 rows of one device no expert is named by more than 48 rows, a bound that some block reaches. swap_flags[0] is 1; the other entries are 0 or 1.
All inputs are finite; a program needn't handle non-finite values.
Results may differ from the reference program's by a relative error of at most 0.0057.
Values may be sent and summed in bfloat16 or wider, within the bound.
A program may use at most 64 MiB of HBM per device.

```python
import math
import jax
import jax.numpy as jnp
import numpy as np
from jax import lax

D = 2048
HID = 768
TOP = 8
TOK_DEV = 64
EXPERTS = 16
HALF = 8
MOST = 48
TOKENS = 2048
N_EXPERT = 16
N_DP = 2


def draw_swap_flags(key, part):
    random_bits = jax.random.randint(key, (HALF,), 0, 2, dtype=jnp.int32)
    return jnp.where(jnp.arange(HALF, dtype=jnp.int32) == 0, 1, random_bits).astype(jnp.int32)


def levels(stream_key, extent, cuts, smallest, largest):
    def one(axis_at, shards_of):
        heights = jax.random.uniform(jax.random.fold_in(jax.random.fold_in(stream_key, 6), axis_at), (shards_of,), jnp.float32, smallest / len(cuts), largest / len(cuts))
        return jnp.repeat(jnp.exp(heights), extent[axis_at] // shards_of).reshape((-1,) + (1,) * (len(extent) - axis_at - 1))

    gain = one(*cuts[0])
    for cut in cuts[1:]:
        gain = gain * one(*cut)
    return gain


def assign_block(own_key, own, number, rows, count, top, bound, lean):
    sequence = jax.random.permutation(own_key, count)
    crowded, common = portions_of(count, rows * top, bound, lean, True), portions_of(count, rows * top, bound, lean, False)
    places = jnp.arange(count)

    def named(tallies, turn):
        used = int((tallies > 0).sum())
        fixed = max(1, used // 4)
        passed = fixed + (places - fixed + turn * (used - fixed)) % max(1, count - fixed)
        return jnp.zeros((count,), jnp.int32).at[sequence[jnp.where(places < fixed, places, passed)]].set(jnp.asarray(tallies, jnp.int32))

    tallies = jnp.where(number % 4 == 0, named(crowded, number // 4), named(common, number - number // 4 - 1))
    mixed = jax.random.permutation(jax.random.fold_in(own, 3), count)
    giver, taker = mixed[0:count // 2 * 2:2], mixed[1:count // 2 * 2:2]
    room = jnp.minimum(tallies[giver] - 1, bound - tallies[taker]) // 2
    room = jnp.where((giver == sequence[0]) | (taker == sequence[0]) | (tallies[taker] == 0), 0, jnp.maximum(room, 0))
    passed = jax.random.randint(jax.random.fold_in(own, 4), (count // 2,), 0, 1 << 20) % (room + 1)
    tallies = tallies.at[giver].add(-passed).at[taker].add(passed)
    labels = jnp.searchsorted(jnp.cumsum(tallies), jnp.arange(rows * top), side="right").astype(jnp.int32)
    table = labels.reshape(top, rows).T
    table = table[jax.random.permutation(jax.random.fold_in(own, 1), rows)]
    turn = jax.random.randint(jax.random.fold_in(own, 2), (rows, 1), 0, top)
    return jnp.take_along_axis(table, (jnp.arange(top)[None, :] + turn) % top, axis=1)


def portions_of(number_of, total, most, slope, full):
    loads = [(1 << 20) // math.isqrt(standing ** slope) + 1 for standing in range(1, number_of + 1)]
    largest = most if full else min(most, max(-(-total // number_of), total * loads[0] // sum(loads)))
    least = 1 if total - largest >= number_of - 1 else 0
    holding, spare = [largest] + [least] * (number_of - 1), total - largest - least * (number_of - 1)
    while spare > 0:
        candidates = [i for i in range(1, number_of) if holding[i] < largest] or [i for i in range(1, number_of) if holding[i] < most]
        mass, budget = sum([loads[i] for i in candidates]), spare
        for i in candidates:
            more = min(most - holding[i], max(1, budget * loads[i] // mass), spare)
            holding[i] = holding[i] + more
            spare = spare - more
    return np.array(holding)


def gaussian(own_key, extent, spread, bound, split=(), kind=jnp.bfloat16):
    drawn = spread * jax.random.normal(own_key, extent, jnp.float32)
    if split:
        drawn = drawn * levels(own_key, extent, split, -0.22, 0.18)
    return jnp.clip(drawn, -bound, bound).astype(kind)


def setup_inputs(seed: int = 0) -> dict:
    key_of = jax.random.split(jax.random.key(seed), 8)
    tokens = gaussian(key_of[0], (TOKENS, D), 1.0, 6.0, ((0, 32),))
    expert_ids_keys = jax.random.split(jax.random.fold_in(key_of[1], 1), TOKENS // TOK_DEV)
    expert_ids_turns = jax.random.permutation(jax.random.fold_in(key_of[1], 3), TOKENS // TOK_DEV)
    expert_ids = jax.vmap(lambda own, number: assign_block(jax.random.fold_in(key_of[1], 2), own, number, TOK_DEV, EXPERTS, TOP, MOST, 2))(expert_ids_keys, expert_ids_turns).reshape((TOKENS, TOP))
    gate_probs = jnp.clip(jnp.exp(math.log(1.0) - 2.9957323 * jax.random.uniform(key_of[2], (TOKENS, TOP), jnp.float32) ** levels(key_of[2], (TOKENS, TOP), ((0, 32),), -0.2, 0.2)), 0.05, 1.0)
    swap_flags = draw_swap_flags(jax.random.fold_in(key_of[7], 71), 0)
    w_gate = gaussian(key_of[4], (EXPERTS, D, HID), D ** -0.5, 0.125, ((0, 16), (1, 2)))
    w_up = gaussian(key_of[5], (EXPERTS, D, HID), D ** -0.5, 0.125, ((0, 16), (1, 2)))
    w_down = gaussian(key_of[6], (EXPERTS, HID, D), HID ** -0.5, 0.21875, ((0, 16), (2, 2)))
    return {"tokens": tokens, "expert_ids": expert_ids, "gate_probs": gate_probs, "swap_flags": swap_flags, "w_gate": w_gate, "w_up": w_up, "w_down": w_down}


def reference(tokens, expert_ids, gate_probs, swap_flags, w_gate, w_up, w_down):
    half_span = EXPERTS // 2
    shares = gate_probs / jnp.sum(gate_probs, axis=1, keepdims=True)
    in_lower = expert_ids < half_span
    base_expert = jnp.where(in_lower, expert_ids, expert_ids - half_span).astype(jnp.int32)
    flagged = swap_flags[base_expert] == 1
    partner = jnp.where(in_lower, expert_ids + half_span, expert_ids - half_span)
    holder = jnp.where(flagged, partner, expert_ids).astype(jnp.int32)
    flat_holder = holder.reshape(-1)
    pair_count = flat_holder.shape[0]
    pair_token = (jnp.arange(pair_count, dtype=jnp.int32) // TOP).astype(jnp.int32)
    flat_share = shares.reshape(-1)
    sorted_pairs = jnp.argsort(flat_holder, stable=True).astype(jnp.int32)
    counts = jnp.sum((flat_holder[:, None] == jnp.arange(EXPERTS, dtype=jnp.int32)[None, :]).astype(jnp.int32), axis=0)
    starts = (jnp.cumsum(counts) - counts).astype(jnp.int32)
    capacity = MOST * N_EXPERT * N_DP
    padded_pairs = jnp.concatenate([sorted_pairs, jnp.zeros((capacity,), jnp.int32)])

    def per_expert(totals, expert_id):
        picked = lax.dynamic_slice_in_dim(padded_pairs, starts[expert_id], capacity)
        is_live = jnp.arange(capacity, dtype=jnp.int32) < counts[expert_id]
        token_rows = pair_token[picked]
        gathered = tokens[token_rows]
        gate_sum = jnp.dot(gathered, w_gate[expert_id], preferred_element_type=jnp.float32)
        up_sum = jnp.dot(gathered, w_up[expert_id], preferred_element_type=jnp.float32)
        hidden = (jax.nn.silu(gate_sum) * up_sum).astype(jnp.bfloat16)
        expert_rows = jnp.dot(hidden, w_down[expert_id], preferred_element_type=jnp.float32).astype(jnp.bfloat16)
        factor = jnp.where(is_live, flat_share[picked], jnp.zeros_like(flat_share[picked]))
        totals = totals.at[token_rows].add(factor[:, None] * expert_rows.astype(jnp.float32))
        return totals, None

    totals, _ = lax.scan(per_expert, jnp.zeros((TOKENS, D), jnp.float32), jnp.arange(EXPERTS, dtype=jnp.int32))
    return totals.astype(jnp.bfloat16)
```

```python
import jax
import jax.numpy as jnp
from jax import lax
from jax.sharding import PartitionSpec as P


def on_device(tokens, expert_ids, gate_probs, swap_flags, w_gate, w_up, w_down):
    axis_size = lax.axis_size("expert")
    own_index = lax.axis_index("expert")
    half_span = axis_size // 2
    shares = gate_probs / jnp.sum(gate_probs, axis=1, keepdims=True)
    experts = jnp.arange(axis_size, dtype=jnp.int32)
    dense = jnp.sum(
        jnp.where(expert_ids[:, :, None] == experts[None, None, :], shares[:, :, None], 0.0), axis=1
    )
    lower = own_index < half_span
    own_base = jnp.where(lower, own_index, own_index - half_span)
    own_flag = (
        jnp.sum(jnp.where(jnp.arange(half_span, dtype=jnp.int32) == own_base, swap_flags, 0)) == 1
    )
    served = jnp.where(
        own_flag, jnp.where(lower, own_index + half_span, own_index - half_span), own_index
    )
    rows = lax.all_gather(tokens, "expert", axis=0, tiled=True)
    dense_all = lax.all_gather(dense, "expert", axis=0, tiled=True)
    factor = jnp.sum(jnp.where(experts[None, :] == served, dense_all, 0.0), axis=1)
    gate_next = jnp.dot(
        rows,
        lax.all_gather(w_gate, "dp", axis=1, tiled=True)[0],
        preferred_element_type=jnp.float32,
    )
    up_next = jnp.dot(
        rows,
        lax.all_gather(w_up, "dp", axis=1, tiled=True)[0],
        preferred_element_type=jnp.float32,
    )
    hidden = (jax.nn.silu(gate_next) * up_next).astype(jnp.bfloat16)
    produced = jnp.dot(
        hidden,
        lax.all_gather(w_down, "dp", axis=2, tiled=True)[0],
        preferred_element_type=jnp.float32,
    ).astype(jnp.bfloat16)
    partial = (factor[:, None] * produced.astype(jnp.float32)).astype(jnp.bfloat16)
    return lax.psum_scatter(partial, "expert", scatter_dimension=0, tiled=True)


def solution(mesh):
    placed = (
        P(("expert", "dp"), None),
        P(("expert", "dp"), None),
        P(("expert", "dp"), None),
        P(),
        P("expert", "dp", None),
        P("expert", "dp", None),
        P("expert", None, "dp"),
    )
    return jax.shard_map(
        on_device, mesh=mesh, in_specs=placed, out_specs=P(("expert", "dp"), None), check_vma=False
    )
```

```python
import functools

import jax
import jax.numpy as jnp
from jax import lax
from jax.experimental import pallas as pl
from jax.experimental.pallas import tpu as pltpu
from jax.sharding import PartitionSpec as P

MESH = pl.DeviceIdType.MESH


def flipped(index, bit):
    return index + bit * (1 - 2 * lax.rem(lax.div(index, bit), 2))


def slot_of(mask, deep):
    return (mask % 4) * deep + mask // 4


def level_of(mask, order):
    return max([i for i, bit in enumerate(order) if mask & bit], default=-1)


def fused_kernel(
    n,
    flags_ref,
    ids_ref,
    probs_ref,
    tokens_ref,
    gate_ref,
    up_ref,
    down_ref,
    out_ref,
    rows_buf,
    gate_buf,
    up_buf,
    down_buf,
    table_buf,
    hidden_buf,
    total_buf,
    leave_buf,
    land_buf,
    weight_sems,
    peer_send,
    peer_recv,
    own_sems,
    row_send,
    row_recv,
    table_send,
    table_recv,
    sum_send,
    sum_recv,
):
    me = lax.axis_index("expert")
    core = lax.axis_index("dp")
    top, count = ids_ref.shape
    width = rows_buf.shape[-1]
    hid = hidden_buf.shape[1]
    deep = n // 4
    line = [1 << i for i in range(2, n.bit_length() - 1)]
    orders = (line + [1, 2], line + [2, 1])
    bits = line + [1, 2]
    target = {bit: {"expert": flipped(me, bit)} for bit in bits}
    peer = {"dp": 1 - core}

    barrier = pltpu.get_barrier_semaphore()
    for device in [target[bit] for bit in bits] + [peer]:
        pl.semaphore_signal(barrier, inc=1, device_id=device, device_id_type=MESH)

    own_weights = [
        pltpu.make_async_copy(src.at[0], dst.at[core], weight_sems.at[i])
        for i, (src, dst) in enumerate(
            ((gate_ref, gate_buf), (up_ref, up_buf), (down_ref, down_buf))
        )
    ]
    own_rows = [
        pltpu.make_async_copy(
            tokens_ref.at[:, pl.ds(half * width, width)], rows_buf.at[half, 0], own_sems.at[half]
        )
        for half in range(2)
    ]
    for copy in own_rows + own_weights:
        copy.start()

    probs = probs_ref[...]
    shares = probs / jnp.sum(probs, axis=0, keepdims=True)
    row = lax.broadcasted_iota(jnp.int32, (n, count), 0)
    base = jnp.where(row < n // 2, row, row - n // 2)
    flag = jnp.zeros((n, count), jnp.int32)
    for j in range(n // 2):
        flag = jnp.where(base == j, flags_ref[j], flag)
    other = jnp.where(row < n // 2, row + n // 2, row - n // 2)
    served = jnp.where(flag == 1, other, row)
    table = jnp.zeros((n, count), jnp.float32)
    for k in range(top):
        table = table + jnp.where(ids_ref[k : k + 1, :] == served, shares[k : k + 1, :], 0.0)
    table_buf[0] = table

    pl.semaphore_wait(barrier, len(bits) + 1)

    def row_copy(half, mask, bit):
        there = mask ^ bit
        slot = slot_of(there, deep)
        src = rows_buf.at[half, slot_of(mask, deep)]
        if mask == 0:
            src = tokens_ref.at[:, pl.ds(half * width, width)]
        return pltpu.make_async_remote_copy(
            src_ref=src,
            dst_ref=rows_buf.at[half, slot],
            send_sem=row_send.at[half, slot],
            recv_sem=row_recv.at[half, slot],
            device_id=target[bit],
            device_id_type=MESH,
        )

    def table_copy(mask, bit):
        slot = slot_of(mask ^ bit, deep)
        return pltpu.make_async_remote_copy(
            src_ref=table_buf.at[slot_of(mask, deep)],
            dst_ref=table_buf.at[slot],
            send_sem=table_send.at[slot],
            recv_sem=table_recv.at[slot],
            device_id=target[bit],
            device_id_type=MESH,
        )

    sent = []

    def start(copy):
        copy.start()
        sent.append(copy)

    def arrival(half, mask):
        bit = orders[half][level_of(mask, orders[half])]
        return row_copy(half, mask ^ bit, bit)

    arrived = set()

    def take(half, mask):
        if mask == 0 or (half, mask) in arrived:
            return
        arrived.add((half, mask))
        order = orders[half]
        level = level_of(mask, order)
        arrival(half, mask).wait_recv()
        if half == 0:
            table_copy(mask ^ order[level], order[level]).wait_recv()
        for bit in order[level + 1 :]:
            if half == 0:
                start(table_copy(mask, bit))
            start(row_copy(half, mask, bit))

    for bit in bits:
        start(table_copy(0, bit))
    for bit in line:
        for half in range(2):
            start(row_copy(half, 0, bit))
        if bit == line[0]:
            start(row_copy(0, 0, 1))
            start(row_copy(1, 0, 2))
    peer_weights = []
    for i, (src, dst) in enumerate(((gate_ref, gate_buf), (up_ref, up_buf), (down_ref, down_buf))):
        copy = pltpu.make_async_remote_copy(
            src_ref=src.at[0],
            dst_ref=dst.at[core],
            send_sem=peer_send.at[i],
            recv_sem=peer_recv.at[i],
            device_id=peer,
            device_id_type=MESH,
        )
        copy.start()
        peer_weights.append(copy)
    start(row_copy(0, 0, 2))
    start(row_copy(1, 0, 1))

    def sum_copy(half, mask):
        order = orders[half]
        bit = order[level_of(mask, order)]
        slot = slot_of(mask, deep)
        return pltpu.make_async_remote_copy(
            src_ref=leave_buf.at[half, slot],
            dst_ref=land_buf.at[half, slot],
            send_sem=sum_send.at[half, slot],
            recv_sem=sum_recv.at[half, slot],
            device_id=target[bit],
            device_id_type=MESH,
        )

    square_row = lax.broadcasted_iota(jnp.int32, (count, count), 0)
    square_column = lax.broadcasted_iota(jnp.int32, (count, count), 1)

    def factor_of(slot):
        mine = jnp.sum(jnp.where(row == me, table_buf[slot], 0.0), axis=0, keepdims=True)
        return jnp.sum(jnp.where(square_row == square_column, mine, 0.0), axis=1, keepdims=True)

    tile = 256

    def compute(batch):
        first = batch * deep
        chunk = deep * count

        def hidden_step(j, carry):
            columns = pl.ds(pl.multiple_of(j * tile, tile), tile)
            gate = jnp.zeros((chunk, tile), jnp.float32)
            up = jnp.zeros((chunk, tile), jnp.float32)
            for half in range(2):
                x = rows_buf[half, first : first + deep].reshape(chunk, width)
                gate = gate + jnp.dot(
                    x, gate_buf[half, :, columns], preferred_element_type=jnp.float32
                )
                up = up + jnp.dot(x, up_buf[half, :, columns], preferred_element_type=jnp.float32)
            silu = gate / (1.0 + jnp.exp(-gate))
            hidden_buf[:, columns] = (silu * up).astype(jnp.bfloat16)
            return carry

        lax.fori_loop(0, hid // tile, hidden_step, 0)
        factors = jnp.concatenate([factor_of(first + i) for i in range(deep)], axis=0)
        halves = (1, 0) if batch == 1 else (0, 1)
        for half in halves:
            final = level_of(batch, orders[half]) == len(bits) - 1

            def down_step(j, carry, half=half, final=final):
                columns = pl.ds(pl.multiple_of(j * tile, tile), tile)
                made = jnp.dot(
                    hidden_buf[...],
                    down_buf[half, :, columns],
                    preferred_element_type=jnp.float32,
                ).astype(jnp.bfloat16)
                part = made.astype(jnp.float32) * factors
                for i in range(deep):
                    block = part[i * count : (i + 1) * count]
                    if final:
                        leave_buf[half, first + i, :, columns] = block.astype(jnp.bfloat16)
                    else:
                        total_buf[half, first + i, :, columns] = block
                return carry

            lax.fori_loop(0, width // tile, down_step, 0)
            if final:
                for high in range(deep - 1, -1, -1):
                    start(sum_copy(half, high * 4 + batch))

    highs = list(range(deep))
    for high in highs[1:]:
        for half in range(2):
            take(half, high * 4)
        take(0, (high - 1) * 4 + 1)
        take(1, (high - 1) * 4 + 2)
    for copy in own_rows + own_weights:
        copy.wait()
    for copy in peer_weights:
        copy.wait_recv()
    take(0, highs[-1] * 4 + 1)
    take(1, highs[-1] * 4 + 2)
    compute(0)
    for batch in (1, 2, 3):
        for high in highs:
            for half in range(2):
                take(half, high * 4 + batch)
        compute(batch)

    def gathered(half, mask):
        order = orders[half]
        total = total_buf[half, slot_of(mask, deep)]
        for bit in reversed(order[level_of(mask, order) + 1 :]):
            sum_copy(half, mask ^ bit).wait_recv()
            total = total + land_buf[half, slot_of(mask ^ bit, deep)].astype(jnp.float32)
        return total

    for high in reversed(highs):
        for half in range(2):
            mask = high * 4 + orders[half][-2]
            leave_buf[half, slot_of(mask, deep)] = gathered(half, mask).astype(jnp.bfloat16)
            start(sum_copy(half, mask))
    for high in reversed(highs):
        for half in range(2):
            mask = high * 4
            if mask:
                leave_buf[half, slot_of(mask, deep)] = gathered(half, mask).astype(jnp.bfloat16)
                start(sum_copy(half, mask))
            else:
                out_ref[:, half * width : (half + 1) * width] = gathered(half, 0).astype(
                    jnp.bfloat16
                )
    for copy in sent + peer_weights:
        copy.wait_send()


def in_one_kernel(tokens, expert_ids, gate_probs, swap_flags, w_gate, w_up, w_down):
    n = lax.axis_size("expert")
    count, model = tokens.shape
    width = model // 2
    hid = w_gate.shape[2]
    deep = n // 4
    any_spec = pl.BlockSpec(memory_space=pl.ANY)
    vmem_spec = pl.BlockSpec(memory_space=pltpu.VMEM)
    dma = pltpu.SemaphoreType.DMA
    return pl.pallas_call(
        functools.partial(fused_kernel, n),
        out_shape=jax.ShapeDtypeStruct((count, model), jnp.bfloat16),
        in_specs=[pl.BlockSpec(memory_space=pltpu.SMEM), vmem_spec, vmem_spec] + [any_spec] * 4,
        out_specs=vmem_spec,
        scratch_shapes=[
            pltpu.VMEM((2, n, count, width), jnp.bfloat16),
            pltpu.VMEM((2, width, hid), jnp.bfloat16),
            pltpu.VMEM((2, width, hid), jnp.bfloat16),
            pltpu.VMEM((2, hid, width), jnp.bfloat16),
            pltpu.VMEM((n, n, count), jnp.float32),
            pltpu.VMEM((deep * count, hid), jnp.bfloat16),
            pltpu.VMEM((2, n, count, width), jnp.float32),
            pltpu.VMEM((2, n, count, width), jnp.bfloat16),
            pltpu.VMEM((2, n, count, width), jnp.bfloat16),
            dma((3,)),
            dma((3,)),
            dma((3,)),
            dma((2,)),
            dma((2, n)),
            dma((2, n)),
            dma((n,)),
            dma((n,)),
            dma((2, n)),
            dma((2, n)),
        ],
        compiler_params=pltpu.CompilerParams(
            collective_id=0, has_side_effects=True, vmem_limit_bytes=48 << 20
        ),
    )(swap_flags, expert_ids.T, gate_probs.T, tokens, w_gate, w_up, w_down)


def kernel_fits(mesh):
    n = mesh.shape["expert"]
    return mesh.shape["dp"] == 2 and n in (8, 16)


def on_device(tokens, expert_ids, gate_probs, swap_flags, w_gate, w_up, w_down):
    axis_size = lax.axis_size("expert")
    own_index = lax.axis_index("expert")
    half_span = axis_size // 2
    shares = gate_probs / jnp.sum(gate_probs, axis=1, keepdims=True)
    experts = jnp.arange(axis_size, dtype=jnp.int32)
    dense = jnp.sum(
        jnp.where(expert_ids[:, :, None] == experts[None, None, :], shares[:, :, None], 0.0), axis=1
    )
    lower = own_index < half_span
    own_base = jnp.where(lower, own_index, own_index - half_span)
    own_flag = (
        jnp.sum(jnp.where(jnp.arange(half_span, dtype=jnp.int32) == own_base, swap_flags, 0)) == 1
    )
    served = jnp.where(
        own_flag, jnp.where(lower, own_index + half_span, own_index - half_span), own_index
    )
    rows = lax.all_gather(tokens, "expert", axis=0, tiled=True)
    dense_all = lax.all_gather(dense, "expert", axis=0, tiled=True)
    factor = jnp.sum(jnp.where(experts[None, :] == served, dense_all, 0.0), axis=1)
    gate_next = jnp.dot(
        rows,
        lax.all_gather(w_gate, "dp", axis=1, tiled=True)[0],
        preferred_element_type=jnp.float32,
    )
    up_next = jnp.dot(
        rows,
        lax.all_gather(w_up, "dp", axis=1, tiled=True)[0],
        preferred_element_type=jnp.float32,
    )
    hidden = (jax.nn.silu(gate_next) * up_next).astype(jnp.bfloat16)
    produced = jnp.dot(
        hidden,
        lax.all_gather(w_down, "dp", axis=2, tiled=True)[0],
        preferred_element_type=jnp.float32,
    ).astype(jnp.bfloat16)
    partial = (factor[:, None] * produced.astype(jnp.float32)).astype(jnp.bfloat16)
    return lax.psum_scatter(partial, "expert", scatter_dimension=0, tiled=True)


def solution(mesh):
    placed = (
        P(("expert", "dp"), None),
        P(("expert", "dp"), None),
        P(("expert", "dp"), None),
        P(),
        P("expert", "dp", None),
        P("expert", "dp", None),
        P("expert", None, "dp"),
    )
    return jax.shard_map(
        in_one_kernel if kernel_fits(mesh) else on_device,
        mesh=mesh, in_specs=placed, out_specs=P(("expert", "dp"), None), check_vma=False
    )
```

```python
import functools

import jax
import jax.numpy as jnp
from jax import lax
from jax.experimental import pallas as pl
from jax.experimental.pallas import tpu as pltpu
from jax.sharding import PartitionSpec as P

MESH = pl.DeviceIdType.MESH


def flipped(index, bit):
    return index + bit * (1 - 2 * lax.rem(lax.div(index, bit), 2))


def slot_of(mask, deep):
    return (mask % 4) * deep + mask // 4


def level_of(mask, order):
    return max([i for i, bit in enumerate(order) if mask & bit], default=-1)


def fused_kernel(
    n,
    flags_ref,
    ids_ref,
    probs_ref,
    tokens_ref,
    gate_ref,
    up_ref,
    down_ref,
    out_ref,
    rows_buf,
    gate_buf,
    up_buf,
    down_buf,
    table_buf,
    hidden_buf,
    total_buf,
    leave_buf,
    land_buf,
    weight_sems,
    peer_send,
    peer_recv,
    own_sems,
    row_send,
    row_recv,
    table_send,
    table_recv,
    sum_send,
    sum_recv,
):
    me = lax.axis_index("expert")
    core = lax.axis_index("dp")
    top, count = ids_ref.shape
    width = rows_buf.shape[-1]
    hid = hidden_buf.shape[1]
    deep = n // 4
    line = [1 << i for i in reversed(range(2, n.bit_length() - 1))]
    orders = (line + [1, 2], line + [2, 1])
    bits = line + [1, 2]
    target = {bit: {"expert": flipped(me, bit)} for bit in bits}
    peer = {"dp": 1 - core}

    barrier = pltpu.get_barrier_semaphore()
    for device in [target[bit] for bit in bits] + [peer]:
        pl.semaphore_signal(barrier, inc=1, device_id=device, device_id_type=MESH)

    own_weights = [
        pltpu.make_async_copy(src.at[0], dst.at[core], weight_sems.at[i])
        for i, (src, dst) in enumerate(
            ((gate_ref, gate_buf), (up_ref, up_buf), (down_ref, down_buf))
        )
    ]
    own_rows = [
        pltpu.make_async_copy(
            tokens_ref.at[:, pl.ds(half * width, width)], rows_buf.at[half, 0], own_sems.at[half]
        )
        for half in range(2)
    ]
    for copy in own_rows + own_weights:
        copy.start()

    probs = probs_ref[...]
    shares = probs / jnp.sum(probs, axis=0, keepdims=True)
    row = lax.broadcasted_iota(jnp.int32, (n, count), 0)
    base = jnp.where(row < n // 2, row, row - n // 2)
    flag = jnp.zeros((n, count), jnp.int32)
    for j in range(n // 2):
        flag = jnp.where(base == j, flags_ref[j], flag)
    other = jnp.where(row < n // 2, row + n // 2, row - n // 2)
    served = jnp.where(flag == 1, other, row)
    table = jnp.zeros((n, count), jnp.float32)
    for k in range(top):
        table = table + jnp.where(ids_ref[k : k + 1, :] == served, shares[k : k + 1, :], 0.0)
    table_buf[0] = table

    pl.semaphore_wait(barrier, len(bits) + 1)

    def row_copy(half, mask, bit):
        there = mask ^ bit
        slot = slot_of(there, deep)
        src = rows_buf.at[half, slot_of(mask, deep)]
        if mask == 0:
            src = tokens_ref.at[:, pl.ds(half * width, width)]
        return pltpu.make_async_remote_copy(
            src_ref=src,
            dst_ref=rows_buf.at[half, slot],
            send_sem=row_send.at[half, slot],
            recv_sem=row_recv.at[half, slot],
            device_id=target[bit],
            device_id_type=MESH,
        )

    def table_copy(mask, bit):
        slot = slot_of(mask ^ bit, deep)
        return pltpu.make_async_remote_copy(
            src_ref=table_buf.at[slot_of(mask, deep)],
            dst_ref=table_buf.at[slot],
            send_sem=table_send.at[slot],
            recv_sem=table_recv.at[slot],
            device_id=target[bit],
            device_id_type=MESH,
        )

    sent = []

    def start(copy):
        copy.start()
        sent.append(copy)

    def arrival(half, mask):
        bit = orders[half][level_of(mask, orders[half])]
        return row_copy(half, mask ^ bit, bit)

    arrived = set()

    def take(half, mask):
        if mask == 0 or (half, mask) in arrived:
            return
        arrived.add((half, mask))
        order = orders[half]
        level = level_of(mask, order)
        arrival(half, mask).wait_recv()
        if half == 0:
            table_copy(mask ^ order[level], order[level]).wait_recv()
        for bit in order[level + 1 :]:
            if half == 0:
                start(table_copy(mask, bit))
            start(row_copy(half, mask, bit))

    for bit in bits:
        start(table_copy(0, bit))
    near, far = line[-1], line[:-1]
    start(row_copy(0, 0, near))
    start(row_copy(0, 0, 1))
    start(row_copy(1, 0, 2))
    start(row_copy(1, 0, near))
    peer_weights = []
    for i, (src, dst) in enumerate(((gate_ref, gate_buf), (up_ref, up_buf), (down_ref, down_buf))):
        copy = pltpu.make_async_remote_copy(
            src_ref=src.at[0],
            dst_ref=dst.at[core],
            send_sem=peer_send.at[i],
            recv_sem=peer_recv.at[i],
            device_id=peer,
            device_id_type=MESH,
        )
        copy.start()
        peer_weights.append(copy)

    def sum_copy(half, mask):
        order = orders[half]
        bit = order[level_of(mask, order)]
        slot = slot_of(mask, deep)
        return pltpu.make_async_remote_copy(
            src_ref=leave_buf.at[half, slot],
            dst_ref=land_buf.at[half, slot],
            send_sem=sum_send.at[half, slot],
            recv_sem=sum_recv.at[half, slot],
            device_id=target[bit],
            device_id_type=MESH,
        )

    square_row = lax.broadcasted_iota(jnp.int32, (count, count), 0)
    square_column = lax.broadcasted_iota(jnp.int32, (count, count), 1)

    def factor_of(slot):
        mine = jnp.sum(jnp.where(row == me, table_buf[slot], 0.0), axis=0, keepdims=True)
        return jnp.sum(jnp.where(square_row == square_column, mine, 0.0), axis=1, keepdims=True)

    tile = 256
    highs = list(range(deep))

    def compute(batch):
        first = batch * deep
        chunk = deep * count

        def hidden_step(j, carry):
            columns = pl.ds(pl.multiple_of(j * tile, tile), tile)
            gate = jnp.zeros((chunk, tile), jnp.float32)
            up = jnp.zeros((chunk, tile), jnp.float32)
            for half in range(2):
                x = rows_buf[half, first : first + deep].reshape(chunk, width)
                gate = gate + jnp.dot(
                    x, gate_buf[half, :, columns], preferred_element_type=jnp.float32
                )
                up = up + jnp.dot(x, up_buf[half, :, columns], preferred_element_type=jnp.float32)
            silu = gate / (1.0 + jnp.exp(-gate))
            hidden_buf[:, columns] = (silu * up).astype(jnp.bfloat16)
            return carry

        lax.fori_loop(0, hid // tile, hidden_step, 0)
        factors = jnp.concatenate([factor_of(first + i) for i in range(deep)], axis=0)
        halves = (1, 0) if batch == 1 else (0, 1)
        for half in halves:
            final = level_of(batch, orders[half]) == len(bits) - 1

            def down_step(j, carry, half=half, final=final):
                columns = pl.ds(pl.multiple_of(j * tile, tile), tile)
                made = jnp.dot(
                    hidden_buf[...],
                    down_buf[half, :, columns],
                    preferred_element_type=jnp.float32,
                ).astype(jnp.bfloat16)
                part = made.astype(jnp.float32) * factors
                for i in range(deep):
                    block = part[i * count : (i + 1) * count]
                    if final:
                        leave_buf[half, first + i, :, columns] = block.astype(jnp.bfloat16)
                    else:
                        total_buf[half, first + i, :, columns] = block
                return carry

            lax.fori_loop(0, width // tile, down_step, 0)

    def gathered(half, mask):
        order = orders[half]
        total = total_buf[half, slot_of(mask, deep)]
        for bit in reversed(order[level_of(mask, order) + 1 :]):
            sum_copy(half, mask ^ bit).wait_recv()
            total = total + land_buf[half, slot_of(mask ^ bit, deep)].astype(jnp.float32)
        return total

    def leave(half, mask):
        leave_buf[half, slot_of(mask, deep)] = gathered(half, mask).astype(jnp.bfloat16)
        start(sum_copy(half, mask))

    def take_pair(high):
        take(0, high * 4 + 1)
        take(1, high * 4 + 2)

    take_pair(0)
    take(0, near)
    start(row_copy(1, 0, 1))
    start(row_copy(0, 0, 2))
    take(1, near)
    for bit in far:
        for half in range(2):
            start(row_copy(half, 0, bit))
    line_order = [near // 4] + [high for high in highs[1:] if high != near // 4]
    for last, high in zip([0] + line_order, line_order):
        take(0, high * 4)
        take(1, high * 4)
        if last:
            take_pair(last)
    for copy in own_rows + own_weights:
        copy.wait()
    for copy in peer_weights:
        copy.wait_recv()
    compute(0)
    take_pair(line_order[-1])
    for batch in (1, 2):
        for high in highs:
            for half in range(2):
                take(half, high * 4 + batch)
        compute(batch)
        half = 2 - batch
        for high in reversed(highs):
            start(sum_copy(half, high * 4 + batch))
    for high in highs:
        for half in range(2):
            take(half, high * 4 + 3)
    compute(3)

    back = list(reversed(highs))

    def corner(high):
        for half in range(2):
            start(sum_copy(half, high * 4 + 3))

    def side(high):
        for half in range(2):
            leave(half, high * 4 + orders[half][-2])

    def stem(high):
        for half in range(2):
            if high:
                leave(half, high * 4)
            else:
                out_ref[:, half * width : (half + 1) * width] = gathered(half, 0).astype(
                    jnp.bfloat16
                )

    lead = 2
    for step in range(deep + lead + 2):
        if step < deep:
            corner(back[step])
        if 0 <= step - lead + 1 < deep:
            side(back[step - lead + 1])
        if 0 <= step - lead < deep:
            stem(back[step - lead])
    for copy in sent + peer_weights:
        copy.wait_send()


def in_one_kernel(tokens, expert_ids, gate_probs, swap_flags, w_gate, w_up, w_down):
    n = lax.axis_size("expert")
    count, model = tokens.shape
    width = model // 2
    hid = w_gate.shape[2]
    deep = n // 4
    any_spec = pl.BlockSpec(memory_space=pltpu.HBM)
    vmem_spec = pl.BlockSpec(memory_space=pltpu.VMEM)
    dma = pltpu.SemaphoreType.DMA
    return pl.pallas_call(
        functools.partial(fused_kernel, n),
        out_shape=jax.ShapeDtypeStruct((count, model), jnp.bfloat16),
        in_specs=[pl.BlockSpec(memory_space=pltpu.SMEM), vmem_spec, vmem_spec] + [any_spec] * 4,
        out_specs=vmem_spec,
        scratch_shapes=[
            pltpu.VMEM((2, n, count, width), jnp.bfloat16),
            pltpu.VMEM((2, width, hid), jnp.bfloat16),
            pltpu.VMEM((2, width, hid), jnp.bfloat16),
            pltpu.VMEM((2, hid, width), jnp.bfloat16),
            pltpu.VMEM((n, n, count), jnp.float32),
            pltpu.VMEM((deep * count, hid), jnp.bfloat16),
            pltpu.VMEM((2, n, count, width), jnp.float32),
            pltpu.VMEM((2, n, count, width), jnp.bfloat16),
            pltpu.VMEM((2, n, count, width), jnp.bfloat16),
            dma((3,)),
            dma((3,)),
            dma((3,)),
            dma((2,)),
            dma((2, n)),
            dma((2, n)),
            dma((n,)),
            dma((n,)),
            dma((2, n)),
            dma((2, n)),
        ],
        compiler_params=pltpu.CompilerParams(
            collective_id=0, has_side_effects=True, vmem_limit_bytes=60 << 20
        ),
    )(swap_flags, expert_ids.T, gate_probs.T, tokens, w_gate, w_up, w_down)


def kernel_fits(mesh):
    n = mesh.shape["expert"]
    return mesh.shape["dp"] == 2 and n in (8, 16)


def on_device(tokens, expert_ids, gate_probs, swap_flags, w_gate, w_up, w_down):
    axis_size = lax.axis_size("expert")
    own_index = lax.axis_index("expert")
    half_span = axis_size // 2
    shares = gate_probs / jnp.sum(gate_probs, axis=1, keepdims=True)
    experts = jnp.arange(axis_size, dtype=jnp.int32)
    dense = jnp.sum(
        jnp.where(expert_ids[:, :, None] == experts[None, None, :], shares[:, :, None], 0.0), axis=1
    )
    lower = own_index < half_span
    own_base = jnp.where(lower, own_index, own_index - half_span)
    own_flag = (
        jnp.sum(jnp.where(jnp.arange(half_span, dtype=jnp.int32) == own_base, swap_flags, 0)) == 1
    )
    served = jnp.where(
        own_flag, jnp.where(lower, own_index + half_span, own_index - half_span), own_index
    )
    rows = lax.all_gather(tokens, "expert", axis=0, tiled=True)
    dense_all = lax.all_gather(dense, "expert", axis=0, tiled=True)
    factor = jnp.sum(jnp.where(experts[None, :] == served, dense_all, 0.0), axis=1)
    gate_next = jnp.dot(
        rows,
        lax.all_gather(w_gate, "dp", axis=1, tiled=True)[0],
        preferred_element_type=jnp.float32,
    )
    up_next = jnp.dot(
        rows,
        lax.all_gather(w_up, "dp", axis=1, tiled=True)[0],
        preferred_element_type=jnp.float32,
    )
    hidden = (jax.nn.silu(gate_next) * up_next).astype(jnp.bfloat16)
    produced = jnp.dot(
        hidden,
        lax.all_gather(w_down, "dp", axis=2, tiled=True)[0],
        preferred_element_type=jnp.float32,
    ).astype(jnp.bfloat16)
    partial = (factor[:, None] * produced.astype(jnp.float32)).astype(jnp.bfloat16)
    return lax.psum_scatter(partial, "expert", scatter_dimension=0, tiled=True)


def solution(mesh):
    placed = (
        P(("expert", "dp"), None),
        P(("expert", "dp"), None),
        P(("expert", "dp"), None),
        P(),
        P("expert", "dp", None),
        P("expert", "dp", None),
        P("expert", None, "dp"),
    )
    return jax.shard_map(
        in_one_kernel if kernel_fits(mesh) else on_device,
        mesh=mesh, in_specs=placed, out_specs=P(("expert", "dp"), None), check_vma=False
    )
```

```python
import functools

import jax
import jax.numpy as jnp
from jax import lax
from jax.experimental import pallas as pl
from jax.experimental.pallas import tpu as pltpu
from jax.sharding import PartitionSpec as P

MESH = pl.DeviceIdType.MESH


def flipped(index, bit):
    return index + bit * (1 - 2 * lax.rem(lax.div(index, bit), 2))


def slot_of(mask, deep):
    return (mask % 4) * deep + mask // 4


def level_of(mask, order):
    return max([i for i, bit in enumerate(order) if mask & bit], default=-1)


def fused_kernel(
    n,
    flags_ref,
    ids_ref,
    probs_ref,
    tokens_ref,
    gate_ref,
    up_ref,
    down_ref,
    out_ref,
    rows_buf,
    gate_buf,
    up_buf,
    down_buf,
    table_buf,
    hidden_buf,
    total_buf,
    leave_buf,
    land_buf,
    weight_sems,
    peer_send,
    peer_recv,
    own_sems,
    row_send,
    row_recv,
    table_send,
    table_recv,
    sum_send,
    sum_recv,
):
    me = lax.axis_index("expert")
    core = lax.axis_index("dp")
    top, count = ids_ref.shape
    width = rows_buf.shape[-1]
    hid = hidden_buf.shape[1]
    deep = n // 4
    line = [1 << i for i in reversed(range(2, n.bit_length() - 1))]
    orders = (line + [1, 2], line + [2, 1])
    bits = line + [1, 2]
    target = {bit: {"expert": flipped(me, bit)} for bit in bits}
    peer = {"dp": 1 - core}

    barrier = pltpu.get_barrier_semaphore()
    for device in [target[bit] for bit in bits] + [peer]:
        pl.semaphore_signal(barrier, inc=1, device_id=device, device_id_type=MESH)

    own_weights = [
        pltpu.make_async_copy(src.at[0], dst.at[core], weight_sems.at[i])
        for i, (src, dst) in enumerate(
            ((gate_ref, gate_buf), (up_ref, up_buf), (down_ref, down_buf))
        )
    ]
    own_rows = [
        pltpu.make_async_copy(
            tokens_ref.at[:, pl.ds(half * width, width)], rows_buf.at[half, 0], own_sems.at[half]
        )
        for half in range(2)
    ]
    for copy in own_rows + own_weights:
        copy.start()

    probs = probs_ref[...]
    shares = probs / jnp.sum(probs, axis=0, keepdims=True)
    row = lax.broadcasted_iota(jnp.int32, (n, count), 0)
    base = jnp.where(row < n // 2, row, row - n // 2)
    flag = jnp.zeros((n, count), jnp.int32)
    for j in range(n // 2):
        flag = jnp.where(base == j, flags_ref[j], flag)
    other = jnp.where(row < n // 2, row + n // 2, row - n // 2)
    served = jnp.where(flag == 1, other, row)
    table = jnp.zeros((n, count), jnp.float32)
    for k in range(top):
        table = table + jnp.where(ids_ref[k : k + 1, :] == served, shares[k : k + 1, :], 0.0)
    table_buf[0] = table

    pl.semaphore_wait(barrier, len(bits) + 1)

    def row_copy(half, mask, bit):
        there = mask ^ bit
        slot = slot_of(there, deep)
        src = rows_buf.at[half, slot_of(mask, deep)]
        if mask == 0:
            src = tokens_ref.at[:, pl.ds(half * width, width)]
        return pltpu.make_async_remote_copy(
            src_ref=src,
            dst_ref=rows_buf.at[half, slot],
            send_sem=row_send.at[half, slot],
            recv_sem=row_recv.at[half, slot],
            device_id=target[bit],
            device_id_type=MESH,
        )

    def table_copy(mask, bit):
        slot = slot_of(mask ^ bit, deep)
        return pltpu.make_async_remote_copy(
            src_ref=table_buf.at[slot_of(mask, deep)],
            dst_ref=table_buf.at[slot],
            send_sem=table_send.at[slot],
            recv_sem=table_recv.at[slot],
            device_id=target[bit],
            device_id_type=MESH,
        )

    sent = []

    def start(copy):
        copy.start()
        sent.append(copy)

    def arrival(half, mask):
        bit = orders[half][level_of(mask, orders[half])]
        return row_copy(half, mask ^ bit, bit)

    arrived = set()

    def take(half, mask):
        if mask == 0 or (half, mask) in arrived:
            return
        arrived.add((half, mask))
        order = orders[half]
        level = level_of(mask, order)
        arrival(half, mask).wait_recv()
        if half == 0:
            table_copy(mask ^ order[level], order[level]).wait_recv()
        for bit in order[level + 1 :]:
            if half == 0:
                start(table_copy(mask, bit))
            start(row_copy(half, mask, bit))

    for bit in bits:
        start(table_copy(0, bit))
    near, far = line[-1], line[:-1]
    start(row_copy(0, 0, near))
    start(row_copy(0, 0, 1))
    start(row_copy(1, 0, 2))
    start(row_copy(1, 0, near))
    start(row_copy(0, 0, far[0]))
    peer_weights = []
    for i, (src, dst) in enumerate(((gate_ref, gate_buf), (up_ref, up_buf), (down_ref, down_buf))):
        copy = pltpu.make_async_remote_copy(
            src_ref=src.at[0],
            dst_ref=dst.at[core],
            send_sem=peer_send.at[i],
            recv_sem=peer_recv.at[i],
            device_id=peer,
            device_id_type=MESH,
        )
        copy.start()
        peer_weights.append(copy)

    def sum_copy(half, mask):
        order = orders[half]
        bit = order[level_of(mask, order)]
        slot = slot_of(mask, deep)
        return pltpu.make_async_remote_copy(
            src_ref=leave_buf.at[half, slot],
            dst_ref=land_buf.at[half, slot],
            send_sem=sum_send.at[half, slot],
            recv_sem=sum_recv.at[half, slot],
            device_id=target[bit],
            device_id_type=MESH,
        )

    square_row = lax.broadcasted_iota(jnp.int32, (count, count), 0)
    square_column = lax.broadcasted_iota(jnp.int32, (count, count), 1)

    def factor_of(slot):
        mine = jnp.sum(jnp.where(row == me, table_buf[slot], 0.0), axis=0, keepdims=True)
        return jnp.sum(jnp.where(square_row == square_column, mine, 0.0), axis=1, keepdims=True)

    tile = 256
    highs = list(range(deep))

    def compute(batch):
        first = batch * deep
        chunk = deep * count

        def hidden_step(j, carry):
            columns = pl.ds(pl.multiple_of(j * tile, tile), tile)
            gate = jnp.zeros((chunk, tile), jnp.float32)
            up = jnp.zeros((chunk, tile), jnp.float32)
            for half in range(2):
                x = rows_buf[half, first : first + deep].reshape(chunk, width)
                gate = gate + jnp.dot(
                    x, gate_buf[half, :, columns], preferred_element_type=jnp.float32
                )
                up = up + jnp.dot(x, up_buf[half, :, columns], preferred_element_type=jnp.float32)
            silu = gate / (1.0 + jnp.exp(-gate))
            hidden_buf[:, columns] = (silu * up).astype(jnp.bfloat16)
            return carry

        lax.fori_loop(0, hid // tile, hidden_step, 0)
        factors = jnp.concatenate([factor_of(first + i) for i in range(deep)], axis=0)
        halves = (1, 0) if batch == 1 else (0, 1)
        for half in halves:
            final = level_of(batch, orders[half]) == len(bits) - 1

            def down_step(j, carry, half=half, final=final):
                columns = pl.ds(pl.multiple_of(j * tile, tile), tile)
                made = jnp.dot(
                    hidden_buf[...],
                    down_buf[half, :, columns],
                    preferred_element_type=jnp.float32,
                ).astype(jnp.bfloat16)
                part = made.astype(jnp.float32) * factors
                for i in range(deep):
                    block = part[i * count : (i + 1) * count]
                    if final:
                        leave_buf[half, first + i, :, columns] = block.astype(jnp.bfloat16)
                    else:
                        total_buf[half, first + i, :, columns] = block
                return carry

            lax.fori_loop(0, width // tile, down_step, 0)

    def gathered(half, mask):
        order = orders[half]
        total = total_buf[half, slot_of(mask, deep)]
        for bit in reversed(order[level_of(mask, order) + 1 :]):
            sum_copy(half, mask ^ bit).wait_recv()
            total = total + land_buf[half, slot_of(mask ^ bit, deep)].astype(jnp.float32)
        return total

    def leave(half, mask):
        leave_buf[half, slot_of(mask, deep)] = gathered(half, mask).astype(jnp.bfloat16)
        start(sum_copy(half, mask))

    def take_pair(high):
        take(0, high * 4 + 1)
        take(1, high * 4 + 2)

    take_pair(0)
    take(0, near)
    start(row_copy(1, 0, 1))
    start(row_copy(0, 0, 2))
    take(1, near)
    start(row_copy(1, 0, far[0]))
    line_order = [near // 4] + [high for high in highs[1:] if high != near // 4]
    for last, high in zip([0] + line_order, line_order):
        take(0, high * 4)
        take(1, high * 4)
        if last:
            take_pair(last)
    for copy in own_rows + own_weights:
        copy.wait()
    for copy in peer_weights:
        copy.wait_recv()
    compute(0)
    take_pair(line_order[-1])
    for batch in (1, 2):
        for high in highs:
            for half in range(2):
                take(half, high * 4 + batch)
        compute(batch)
        half = 2 - batch
        for high in list(reversed(highs))[:2]:
            start(sum_copy(half, high * 4 + batch))
    for high in highs:
        for half in range(2):
            take(half, high * 4 + 3)
    compute(3)

    back = list(reversed(highs))

    def corner(high):
        for half in range(2):
            start(sum_copy(half, high * 4 + 3))

    def side(high):
        for half in range(2):
            leave(half, high * 4 + orders[half][-2])

    def stem(high):
        for half in range(2):
            if high:
                leave(half, high * 4)
            else:
                out_ref[:, half * width : (half + 1) * width] = gathered(half, 0).astype(
                    jnp.bfloat16
                )

    lead = 2
    for step in range(deep + lead + 2):
        if step < deep:
            corner(back[step])
        if 0 <= step - lead + 1 < deep:
            side(back[step - lead + 1])
        if 2 <= step + 1 < deep:
            for half in range(2):
                start(sum_copy(half, back[step + 1] * 4 + orders[half][-1]))
        if 0 <= step - lead < deep:
            stem(back[step - lead])
    for copy in sent + peer_weights:
        copy.wait_send()


def in_one_kernel(tokens, expert_ids, gate_probs, swap_flags, w_gate, w_up, w_down):
    n = lax.axis_size("expert")
    count, model = tokens.shape
    width = model // 2
    hid = w_gate.shape[2]
    deep = n // 4
    any_spec = pl.BlockSpec(memory_space=pltpu.HBM)
    vmem_spec = pl.BlockSpec(memory_space=pltpu.VMEM)
    dma = pltpu.SemaphoreType.DMA
    return pl.pallas_call(
        functools.partial(fused_kernel, n),
        out_shape=jax.ShapeDtypeStruct((count, model), jnp.bfloat16),
        in_specs=[pl.BlockSpec(memory_space=pltpu.SMEM), vmem_spec, vmem_spec] + [any_spec] * 4,
        out_specs=vmem_spec,
        scratch_shapes=[
            pltpu.VMEM((2, n, count, width), jnp.bfloat16),
            pltpu.VMEM((2, width, hid), jnp.bfloat16),
            pltpu.VMEM((2, width, hid), jnp.bfloat16),
            pltpu.VMEM((2, hid, width), jnp.bfloat16),
            pltpu.VMEM((n, n, count), jnp.float32),
            pltpu.VMEM((deep * count, hid), jnp.bfloat16),
            pltpu.VMEM((2, n, count, width), jnp.float32),
            pltpu.VMEM((2, n, count, width), jnp.bfloat16),
            pltpu.VMEM((2, n, count, width), jnp.bfloat16),
            dma((3,)),
            dma((3,)),
            dma((3,)),
            dma((2,)),
            dma((2, n)),
            dma((2, n)),
            dma((n,)),
            dma((n,)),
            dma((2, n)),
            dma((2, n)),
        ],
        compiler_params=pltpu.CompilerParams(
            collective_id=0, has_side_effects=True, vmem_limit_bytes=60 << 20
        ),
    )(swap_flags, expert_ids.T, gate_probs.T, tokens, w_gate, w_up, w_down)


def kernel_fits(mesh):
    n = mesh.shape["expert"]
    return mesh.shape["dp"] == 2 and n in (8, 16)


def on_device(tokens, expert_ids, gate_probs, swap_flags, w_gate, w_up, w_down):
    axis_size = lax.axis_size("expert")
    own_index = lax.axis_index("expert")
    half_span = axis_size // 2
    shares = gate_probs / jnp.sum(gate_probs, axis=1, keepdims=True)
    experts = jnp.arange(axis_size, dtype=jnp.int32)
    dense = jnp.sum(
        jnp.where(expert_ids[:, :, None] == experts[None, None, :], shares[:, :, None], 0.0), axis=1
    )
    lower = own_index < half_span
    own_base = jnp.where(lower, own_index, own_index - half_span)
    own_flag = (
        jnp.sum(jnp.where(jnp.arange(half_span, dtype=jnp.int32) == own_base, swap_flags, 0)) == 1
    )
    served = jnp.where(
        own_flag, jnp.where(lower, own_index + half_span, own_index - half_span), own_index
    )
    rows = lax.all_gather(tokens, "expert", axis=0, tiled=True)
    dense_all = lax.all_gather(dense, "expert", axis=0, tiled=True)
    factor = jnp.sum(jnp.where(experts[None, :] == served, dense_all, 0.0), axis=1)
    gate_next = jnp.dot(
        rows,
        lax.all_gather(w_gate, "dp", axis=1, tiled=True)[0],
        preferred_element_type=jnp.float32,
    )
    up_next = jnp.dot(
        rows,
        lax.all_gather(w_up, "dp", axis=1, tiled=True)[0],
        preferred_element_type=jnp.float32,
    )
    hidden = (jax.nn.silu(gate_next) * up_next).astype(jnp.bfloat16)
    produced = jnp.dot(
        hidden,
        lax.all_gather(w_down, "dp", axis=2, tiled=True)[0],
        preferred_element_type=jnp.float32,
    ).astype(jnp.bfloat16)
    partial = (factor[:, None] * produced.astype(jnp.float32)).astype(jnp.bfloat16)
    return lax.psum_scatter(partial, "expert", scatter_dimension=0, tiled=True)


def solution(mesh):
    placed = (
        P(("expert", "dp"), None),
        P(("expert", "dp"), None),
        P(("expert", "dp"), None),
        P(),
        P("expert", "dp", None),
        P("expert", "dp", None),
        P("expert", None, "dp"),
    )
    return jax.shard_map(
        in_one_kernel if kernel_fits(mesh) else on_device,
        mesh=mesh, in_specs=placed, out_specs=P(("expert", "dp"), None), check_vma=False
    )
```
